32 devices in a mesh: season: 2 (over core), cells: 16 (over z, y, x).
Axes of the slice: x: 2, y: 2, z: 4, core: 2. Of those that a mesh axis runs over, the one named last changes fastest.
Arguments:
- start_adjoint: float32 [2, 8, 32768], P('season', None, 'cells'), may hold values from -6 to 6
- adjoint_tiles: bfloat16 [2, 2, 256, 3, 128, 128], P('season', None, 'cells'), may hold values from -0.21875 to 0.21875
- column_tiles: int32 [2, 2, 256, 3], P('season', None, 'cells'), may hold values from 0 to 255, as said below
- source_jacobian: float32 [2, 2, 8, 8, 32768], P('season', None, None, None, 'cells'), may hold values from -0.9 to 0.9
- obs_owner: int32 [2, 4096, 1], P('season', 'cells'), may hold values from 0 to 15; in each aligned block of 256 rows (0 to 255, 256 to 511, ..., all dimensions but the last counted through in order) at most 32 rows name the same one
- obs_local: int32 [2, 4096], P('season', 'cells'), may hold values from 0 to 2047
- obs_day: int32 [2, 4096], P('season', 'cells'), may hold values from 0 to 1
- obs_tracer: int32 [2, 4096], P('season', 'cells'), may hold values from 0 to 7
- obs_misfit: float32 [2, 4096], P('season', 'cells'), may hold values from -6 to 6
Outputs:
- start_update: float32 [2, 8, 32768], P('season', None, 'cells')
The draws below stay inside these ranges and needn't reach their ends.
Inputs may be any that keep to these rules, and one draw needn't show every extreme that they name: `column_tiles`: entry [s, m, t, 0] equals t; every other entry lies within 8 tiles of t on the closed range of 256 tiles, indices taken modulo 256. `obs_owner`: in each aligned block of 256 observations (the list of one device) no owner is named more than 32 times, a bound that some block reaches.
All inputs are finite; a program needn't handle non-finite values.
Results may differ from the reference program's by a relative error of at most 0.0003.
Values sent between devices are 32-bit elements; how exact they have to be, the bound alone decides.
A program may use at most 64 MiB of HBM per device.

```python
import math
import jax
import jax.numpy as jnp
import numpy as np
from jax import lax

TRACERS = 8
TILE = 128
NB = 3
DAYS = 2
OBS_DEV = 256
REACH = 8
CAP = 32
SEASONS = 2
CELLS_DEV = 2048
TILES = 256
CELLS = 32768
OBS = 4096
N_CELLS = 16


def draw_column_tiles(key, part):
    offsets = jax.random.randint(key, (SEASONS, 2, TILES, NB), -REACH, REACH + 1)
    offsets = offsets.at[:, :, :, 0].set(0)
    offsets = offsets.at[:, :, 0, 1].set(REACH)
    offsets = offsets.at[:, :, 0, 2].set(-REACH)
    row_tiles = jnp.arange(TILES, dtype=jnp.int32)[None, None, :, None]
    return ((row_tiles + offsets) % TILES).astype(jnp.int32)


def place_ends(entries, key, low, largest):
    spot = [jax.random.randint(jax.random.fold_in(key, axis), (), 0, length) for axis, length in enumerate(entries.shape)]
    widest = entries.shape.index(max(entries.shape))
    next_to = spot[:widest] + [(spot[widest] + 1) % entries.shape[widest]] + spot[widest + 1:]
    return entries.at[tuple(spot)].set(low).at[tuple(next_to)].set(largest)


def steps_of(own_key, shape, split, low, largest):
    gain, own = 1.0, jax.random.fold_in(own_key, 6)
    for axis_at, parts in split:
        heights = jnp.exp(jax.random.uniform(jax.random.fold_in(own, axis_at), (parts,), jnp.float32, low / len(split), largest / len(split)))
        gain = gain * jnp.repeat(heights, shape[axis_at] // parts).reshape([-1 if axis == axis_at else 1 for axis in range(len(shape))])
    return gain


def assign_block(key, own, number, rows, amount, top, reach, lean):
    ranking = jax.random.permutation(key, amount)
    crowded, usual = shares(amount, rows * top, reach, lean, True), shares(amount, rows * top, reach, lean, False)
    places = jnp.arange(amount)

    def named(tallies, turn):
        used = int((tallies > 0).sum())
        fixed = max(1, used // 4)
        moved = fixed + (places - fixed + turn * (used - fixed)) % max(1, amount - fixed)
        return jnp.zeros((amount,), jnp.int32).at[ranking[jnp.where(places < fixed, places, moved)]].set(jnp.asarray(tallies, jnp.int32))

    tallies = jnp.where(number % 4 == 0, named(crowded, number // 4), named(usual, number - number // 4 - 1))
    mixed = jax.random.permutation(jax.random.fold_in(own, 3), amount)
    giver, receiver = mixed[0:amount // 2 * 2:2], mixed[1:amount // 2 * 2:2]
    room = jnp.minimum(tallies[giver] - 1, reach - tallies[receiver]) // 2
    room = jnp.where((giver == ranking[0]) | (receiver == ranking[0]) | (tallies[receiver] == 0), 0, jnp.maximum(room, 0))
    moved = jax.random.randint(jax.random.fold_in(own, 4), (amount // 2,), 0, 1 << 20) % (room + 1)
    tallies = tallies.at[giver].add(-moved).at[receiver].add(moved)
    members = jnp.searchsorted(jnp.cumsum(tallies), jnp.arange(rows * top), side="right").astype(jnp.int32)
    listing = members.reshape(top, rows).T
    listing = listing[jax.random.permutation(jax.random.fold_in(own, 1), rows)]
    turn = jax.random.randint(jax.random.fold_in(own, 2), (rows, 1), 0, top)
    return jnp.take_along_axis(listing, (jnp.arange(top)[None, :] + turn) % top, axis=1)


def shares(count, total, most, slope, full):
    weights = [(1 << 20) // math.isqrt(standing ** slope) + 1 for standing in range(1, count + 1)]
    largest = most if full else min(most, max(-(-total // count), total * weights[0] // sum(weights)))
    least = 1 if total - largest >= count - 1 else 0
    holding, rest = [largest] + [least] * (count - 1), total - largest - least * (count - 1)
    while rest > 0:
        candidates = [i for i in range(1, count) if holding[i] < largest] or [i for i in range(1, count) if holding[i] < most]
        pool, budget = sum([weights[i] for i in candidates]), rest
        for i in candidates:
            extra = min(most - holding[i], max(1, budget * weights[i] // pool), rest)
            holding[i] = holding[i] + extra
            rest = rest - extra
    return np.array(holding)


def normal_values(rng, dims, deviation, most, split=(), kind=jnp.bfloat16):
    gain = steps_of(rng, dims, split, -0.22, 0.18) if split else 1.0
    values = jax.random.normal(rng, dims, jnp.float32) * deviation * gain
    return jnp.minimum(jnp.maximum(values, -most), most).astype(kind)


def setup_inputs(seed: int = 0) -> dict:
    splits = jax.random.split(jax.random.key(seed), 10)
    start_adjoint = normal_values(splits[0], (SEASONS, TRACERS, CELLS), 1.0, 6.0, ((0, 2), (2, 16)), jnp.float32)
    adjoint_tiles = normal_values(splits[1], (SEASONS, 2, TILES, NB, TILE, TILE), (2 * TILE * NB) ** -0.5, 0.21875, ((0, 2), (2, 16)))
    column_tiles = draw_column_tiles(jax.random.fold_in(splits[9], 71), 0)
    source_jacobian = normal_values(splits[3], (SEASONS, DAYS, TRACERS, TRACERS, CELLS), 0.15, 0.9, ((0, 2), (4, 16)), jnp.float32)
    obs_owner_keys = jax.random.split(jax.random.fold_in(splits[4], 1), SEASONS * OBS // OBS_DEV)
    obs_owner_turns = jax.random.permutation(jax.random.fold_in(splits[4], 3), SEASONS * OBS // OBS_DEV)
    obs_owner = jax.vmap(lambda own, number: assign_block(jax.random.fold_in(splits[4], 2), own, number, OBS_DEV, N_CELLS, 1, CAP, 2))(obs_owner_keys, obs_owner_turns).reshape((SEASONS, OBS, 1))
    obs_local = place_ends(jax.random.randint(splits[5], (SEASONS, OBS), 0, CELLS_DEV), jax.random.fold_in(splits[5], 1), 0, CELLS_DEV - 1).astype(jnp.int32)
    obs_day = place_ends(jax.random.randint(splits[6], (SEASONS, OBS), 0, DAYS), jax.random.fold_in(splits[6], 1), 0, DAYS - 1).astype(jnp.int32)
    obs_tracer = place_ends(jax.random.randint(splits[7], (SEASONS, OBS), 0, TRACERS), jax.random.fold_in(splits[7], 1), 0, TRACERS - 1).astype(jnp.int32)
    obs_misfit = normal_values(splits[8], (SEASONS, OBS), 1.0, 6.0, ((0, 2), (1, 16)), jnp.float32)
    return dict(start_adjoint=start_adjoint, adjoint_tiles=adjoint_tiles, column_tiles=column_tiles, source_jacobian=source_jacobian, obs_owner=obs_owner, obs_local=obs_local, obs_day=obs_day, obs_tracer=obs_tracer, obs_misfit=obs_misfit)


def apply_matrix(matrix_tiles, column_ids, adjoint_field):
    blocks = adjoint_field.reshape(TRACERS, TILES, TILE)
    picked = jnp.take(blocks, column_ids.reshape(-1), axis=1).reshape(TRACERS, TILES, NB, TILE)
    product = jnp.einsum("tkac,rtkc->rta", matrix_tiles.astype(jnp.float32), picked, precision=lax.Precision.HIGHEST)
    return adjoint_field + product.reshape(TRACERS, CELLS)


def segment_forcing(values, slot_ids):
    return jax.ops.segment_sum(values, slot_ids, num_segments=DAYS * TRACERS * CELLS)


def reference(start_adjoint, adjoint_tiles, column_tiles, source_jacobian, obs_owner, obs_local, obs_day, obs_tracer, obs_misfit):
    end_adjoint = jnp.roll(start_adjoint, -1, axis=0)
    global_cell = (obs_owner[:, :, 0] * CELLS_DEV + obs_local).astype(jnp.int32)
    slot_ids = ((obs_day * TRACERS + obs_tracer) * CELLS + global_cell).astype(jnp.int32)
    forcing = jax.vmap(segment_forcing)(obs_misfit, slot_ids).reshape(SEASONS, DAYS, TRACERS, CELLS)

    def one_segment(inputs):
        adjoint, matrix_tiles, column_ids, jacobian, season_forcing = inputs
        for day_index in reversed(range(DAYS)):
            carried = apply_matrix(matrix_tiles[0], column_ids[0], adjoint)
            coupled = jnp.einsum("jrc,jc->rc", jacobian[day_index], carried, precision=lax.Precision.HIGHEST)
            adjoint = apply_matrix(matrix_tiles[1], column_ids[1], carried) + coupled + season_forcing[day_index]
        return adjoint

    return lax.map(one_segment, (end_adjoint, adjoint_tiles, column_tiles, source_jacobian, forcing))
```

```python
import functools

import jax
import jax.numpy as jnp
from jax import lax
from jax.experimental import pallas as pl
from jax.experimental.pallas import tpu as pltpu
from jax.sharding import PartitionSpec as P

REACH = 8
MESH = pl.DeviceIdType.MESH
F32 = jnp.float32
BF16 = jnp.bfloat16


def dot_nt(a, b):
    return lax.dot_general(a, b, (((1,), (1,)), ((), ())), preferred_element_type=F32)


def kernel(
    seasons,
    peers,
    cols_ref,
    start_ref,
    tiles_hbm,
    jac_hbm,
    owner_ref,
    local_ref,
    day_ref,
    tracer_ref,
    misfit_ref,
    out_ref,
    tiles_vm,
    jac_vm,
    wide,
    packed,
    base,
    obs,
    force,
    load_sem,
    send_sem,
    recv_sem,
    obs_send_sem,
    obs_recv_sem,
):
    s = lax.axis_index("season")
    c = lax.axis_index("cells")
    days, tracers = jac_vm.shape[0], jac_vm.shape[1]
    tiles_here, near = tiles_vm.shape[1], tiles_vm.shape[2]
    rows = tiles_vm.shape[-1]
    cells_here = tiles_here * rows
    halo = REACH * rows
    rounds = 2 * days
    own = slice(halo, halo + cells_here)

    loads = [
        pltpu.make_async_copy(tiles_hbm.at[0, 0], tiles_vm.at[0], load_sem.at[0]),
        pltpu.make_async_copy(tiles_hbm.at[0, 1], tiles_vm.at[1], load_sem.at[1]),
        pltpu.make_async_copy(jac_hbm.at[0], jac_vm, load_sem.at[2]),
    ]
    for load in loads:
        load.start()

    met = {(0, o) for o in range(1, peers)}
    met |= {(ds % seasons, dc % peers) for ds in (1, -1) for dc in (-1, 0, 1)}
    met = sorted(met - {(0, 0)})
    barrier = pltpu.get_barrier_semaphore()
    for ds, dc in met:
        pl.semaphore_signal(
            barrier,
            inc=1,
            device_id=(lax.rem(s + ds, seasons), lax.rem(c + dc, peers)),
            device_id_type=MESH,
        )

    shift = rows.bit_length() - 1
    local = local_ref[...]
    row_key = (local >> shift) * (days * tracers) + day_ref[...] * tracers + tracer_ref[...]
    fields = (
        owner_ref[...].astype(F32),
        row_key.astype(F32),
        (local & (rows - 1)).astype(F32),
        misfit_ref[...],
    )
    lists = local.shape[1] // rows
    pieces = [f[:, i * rows : (i + 1) * rows] for f in fields for i in range(lists)]
    obs[0] = jnp.concatenate(pieces, axis=0)

    left, right = lax.rem(c + peers - 1, peers), lax.rem(c + 1, peers)
    before = lax.rem(s + seasons - 1, seasons)

    def copy(src, r, lanes, season, cell, which):
        return pltpu.make_async_remote_copy(
            src_ref=src,
            dst_ref=wide.at[r, :, lanes],
            send_sem=send_sem.at[r, which],
            recv_sem=recv_sem.at[r, which],
            device_id=(season, cell),
            device_id_type=MESH,
        )

    def halo_copies(r):
        season = before if r == 0 else s
        if r == 0:
            head = start_ref.at[0, :, 0:halo]
            tail = start_ref.at[0, :, cells_here - halo : cells_here]
        else:
            head = wide.at[r, :, halo : 2 * halo]
            tail = wide.at[r, :, cells_here : halo + cells_here]
        return (
            copy(head, r, slice(halo + cells_here, 2 * halo + cells_here), season, left, 0),
            copy(tail, r, slice(0, halo), season, right, 1),
        )

    def obs_copy(o):
        return pltpu.make_async_remote_copy(
            src_ref=obs.at[0],
            dst_ref=obs.at[o],
            send_sem=obs_send_sem.at[o],
            recv_sem=obs_recv_sem.at[o],
            device_id=(s, lax.rem(c + o, peers)),
            device_id_type=MESH,
        )

    sends = [halo_copies(r) for r in range(rounds)]
    body = copy(start_ref.at[0], 0, own, before, c, 2)

    pl.semaphore_wait(barrier, len(met))
    sends[0][0].start()
    sends[0][1].start()
    body.start()

    @pl.loop(1, peers)
    def _(o):
        obs_copy(o).start()

    def pack(r, first, count):
        for t in range(first, first + count):
            v = wide[r, :, at_tile(t)]
            high = v.astype(BF16).astype(F32)
            packed[t] = jnp.concatenate([high, v - high], axis=0).astype(BF16)

    def gather_forcing():
        row_ids = lax.broadcasted_iota(jnp.int32, (force.shape[0], rows), 0).astype(F32)
        lane_ids = lax.broadcasted_iota(jnp.int32, (rows, rows), 0).astype(F32)
        here = c.astype(F32)
        force[...] = jnp.zeros_like(force)

        @pl.loop(0, peers)
        def _(o):
            @pl.when(o > 0)
            def _():
                obs_copy(o).wait_recv()

            block = obs[o]
            slots, values = [], []
            for i in range(lists):
                owner = block[i : i + 1]
                row = jnp.where(owner == here, block[lists + i : lists + i + 1], -1.0)
                lane = block[2 * lists + i : 2 * lists + i + 1]
                misfit = block[3 * lists + i : 3 * lists + i + 1]
                high = misfit.astype(BF16).astype(F32)
                hit = lane_ids == lane
                slots.append(jnp.where(row_ids == row, 1.0, 0.0).astype(BF16))
                values.append(
                    jnp.concatenate(
                        [jnp.where(hit, high, 0.0), jnp.where(hit, misfit - high, 0.0)], axis=0
                    ).astype(BF16)
                )
            force[...] += dot_nt(
                jnp.concatenate(slots, axis=1), jnp.concatenate(values, axis=1)
            )

    def at_tile(t):
        return slice(t * rows, (t + 1) * rows)

    def shifted(t):
        return slice(halo + t * rows, halo + (t + 1) * rows)

    def own_terms(r, day):
        matrix = r % 2
        pack(r, REACH, tiles_here)
        for t in range(tiles_here):
            v = wide[r, :, shifted(t)]
            both = dot_nt(packed[REACH + t], tiles_vm[matrix, t, 0])
            total = v + both[:tracers] + both[tracers:]
            if matrix == 1:
                at = (t * days + day) * tracers
                total += force[at : at + tracers, :rows] + force[at : at + tracers, rows:]
                for j in range(tracers):
                    total += jac_vm[day, j, :, at_tile(t)] * v[j : j + 1]
            base[:, at_tile(t)] = total

    def far_terms(r, chosen):
        matrix = r % 2
        for t in chosen:
            at = (matrix * tiles_here + t) * near
            picks = [packed[cols_ref[at + k]] for k in range(1, near)]
            stored = [tiles_vm[matrix, t, k] for k in range(1, near)]
            both = dot_nt(jnp.concatenate(picks, axis=1), jnp.concatenate(stored, axis=1))
            total = base[:, at_tile(t)] + both[:tracers] + both[tracers:]
            if r == rounds - 1:
                out_ref[0, :, at_tile(t)] = total
            else:
                wide[r + 1, :, shifted(t)] = total

    for r in range(rounds):
        day = days - 1 - r // 2
        if r == 0:
            body.wait_recv()
            loads[0].wait()
        if r == 1:
            loads[1].wait()
            loads[2].wait()
            gather_forcing()
        own_terms(r, day)
        sends[r][1].wait_recv()
        pack(r, 0, REACH)
        far_terms(r, range(0, REACH))
        if r < rounds - 1:
            sends[r + 1][0].start()
        sends[r][0].wait_recv()
        pack(r, REACH + tiles_here, REACH)
        far_terms(r, range(tiles_here - REACH, tiles_here))
        if r < rounds - 1:
            sends[r + 1][1].start()

    for pair in sends:
        for one in pair:
            one.wait_send()
    body.wait_send()

    @pl.loop(1, peers)
    def _(o):
        obs_copy(o).wait_send()


def on_device(
    seasons,
    peers,
    start_adjoint,
    adjoint_tiles,
    column_tiles,
    source_jacobian,
    obs_owner,
    obs_local,
    obs_day,
    obs_tracer,
    obs_misfit,
):
    days, tracers = source_jacobian.shape[1], source_jacobian.shape[2]
    tiles_here, near, rows = adjoint_tiles.shape[2], adjoint_tiles.shape[3], adjoint_tiles.shape[-1]
    cells_here = start_adjoint.shape[2]
    assert tiles_here == 2 * REACH
    wide_cells = cells_here + 2 * REACH * rows
    listed = obs_local.shape[1]
    rounds = 2 * days
    first_tile = lax.axis_index("cells") * tiles_here
    local_tiles = (column_tiles - first_tile + REACH) % (tiles_here * peers)
    vmem = pl.BlockSpec(memory_space=pltpu.VMEM)
    hbm = pl.BlockSpec(memory_space=pl.ANY)
    return pl.pallas_call(
        functools.partial(kernel, seasons, peers),
        out_shape=jax.ShapeDtypeStruct(start_adjoint.shape, F32),
        in_specs=[pl.BlockSpec(memory_space=pltpu.SMEM), hbm, hbm, hbm] + [vmem] * 5,
        out_specs=vmem,
        scratch_shapes=[
            pltpu.VMEM((2, tiles_here, near, rows, rows), BF16),
            pltpu.VMEM((days, tracers, tracers, cells_here), F32),
            pltpu.VMEM((rounds, tracers, wide_cells), F32),
            pltpu.VMEM((tiles_here + 2 * REACH, 2 * tracers, rows), BF16),
            pltpu.VMEM((tracers, cells_here), F32),
            pltpu.VMEM((peers, 4 * listed // rows, rows), F32),
            pltpu.VMEM((tiles_here * days * tracers, 2 * rows), F32),
            pltpu.SemaphoreType.DMA((3,)),
            pltpu.SemaphoreType.DMA((rounds, 3)),
            pltpu.SemaphoreType.DMA((rounds, 3)),
            pltpu.SemaphoreType.DMA((peers,)),
            pltpu.SemaphoreType.DMA((peers,)),
        ],
        compiler_params=pltpu.CompilerParams(collective_id=0, has_side_effects=True),
    )(
        local_tiles.reshape(-1),
        start_adjoint,
        adjoint_tiles,
        source_jacobian,
        obs_owner.reshape(1, listed),
        obs_local,
        obs_day,
        obs_tracer,
        obs_misfit,
    )


def solution(mesh):
    placed = (
        P("season", None, "cells"),
        P("season", None, "cells", None, None, None),
        P("season", None, "cells", None),
        P("season", None, None, None, "cells"),
        P("season", "cells", None),
        P("season", "cells"),
        P("season", "cells"),
        P("season", "cells"),
        P("season", "cells"),
    )
    return jax.shard_map(
        functools.partial(on_device, mesh.shape["season"], mesh.shape["cells"]),
        mesh=mesh,
        in_specs=placed,
        out_specs=P("season", None, "cells"),
        check_vma=False,
    )
```

```python
import functools

import jax
import jax.numpy as jnp
from jax import lax
from jax.experimental import pallas as pl
from jax.experimental.pallas import tpu as pltpu
from jax.sharding import PartitionSpec as P

REACH = 8
PIECES = 2
MESH = pl.DeviceIdType.MESH
F32 = jnp.float32
BF16 = jnp.bfloat16


def dot_nt(a, b):
    return lax.dot_general(a, b, (((1,), (1,)), ((), ())), preferred_element_type=F32)


def kernel(
    seasons,
    peers,
    cols_hbm,
    start_ref,
    tiles_hbm,
    jac_hbm,
    owner_hbm,
    local_hbm,
    day_hbm,
    tracer_hbm,
    misfit_hbm,
    out_hbm,
    cols_ref,
    owner_ref,
    local_ref,
    day_ref,
    tracer_ref,
    misfit_ref,
    out_ref,
    tiles_vm,
    jac_vm,
    wide,
    packed,
    base,
    obs,
    force,
    load_sem,
    store_sem,
    send_sem,
    recv_sem,
    obs_send_sem,
    obs_recv_sem,
):
    s = lax.axis_index("season")
    c = lax.axis_index("cells")
    days, tracers = jac_vm.shape[0], jac_vm.shape[1]
    tiles_here, near = tiles_vm.shape[1], tiles_vm.shape[2]
    rows = tiles_vm.shape[-1]
    cells_here = tiles_here * rows
    halo = REACH * rows
    total_tiles = tiles_here * peers
    piece = halo // PIECES
    step = REACH // PIECES
    rounds = 2 * days
    own = slice(halo, halo + cells_here)

    met = {(0, o) for o in range(1, peers)}
    met |= {(ds % seasons, dc % peers) for ds in (1, -1) for dc in (-1, 0, 1)}
    met = sorted(met - {(0, 0)})
    barrier = pltpu.get_barrier_semaphore()
    for ds, dc in met:
        pl.semaphore_signal(
            barrier,
            inc=1,
            device_id=(lax.rem(s + ds, seasons), lax.rem(c + dc, peers)),
            device_id_type=MESH,
        )

    pairs = (
        (owner_hbm, owner_ref),
        (local_hbm, local_ref),
        (day_hbm, day_ref),
        (tracer_hbm, tracer_ref),
        (misfit_hbm, misfit_ref),
        (cols_hbm, cols_ref),
        (tiles_hbm.at[0, 0], tiles_vm.at[0]),
        (tiles_hbm.at[0, 1], tiles_vm.at[1]),
        (jac_hbm.at[0], jac_vm),
    )
    loads = [pltpu.make_async_copy(a, b, load_sem.at[i]) for i, (a, b) in enumerate(pairs)]
    for load in loads:
        load.start()
    for load in loads[:5]:
        load.wait()

    shift = rows.bit_length() - 1
    local = local_ref[...]
    row_key = (local >> shift) * (days * tracers) + day_ref[...] * tracers + tracer_ref[...]
    fields = (
        owner_ref[...].astype(F32),
        row_key.astype(F32),
        (local & (rows - 1)).astype(F32),
        misfit_ref[...],
    )
    lists = local.shape[1] // rows
    pieces = [f[:, i * rows : (i + 1) * rows] for f in fields for i in range(lists)]
    obs[0] = jnp.concatenate(pieces, axis=0)

    left, right = lax.rem(c + peers - 1, peers), lax.rem(c + 1, peers)
    before = lax.rem(s + seasons - 1, seasons)

    def copy(src, r, lanes, season, cell, which):
        return pltpu.make_async_remote_copy(
            src_ref=src,
            dst_ref=wide.at[r, :, lanes],
            send_sem=send_sem.at[r, which],
            recv_sem=recv_sem.at[r, which],
            device_id=(season, cell),
            device_id_type=MESH,
        )

    def halo_copies(r):
        season = before if r == 0 else s
        copies = []
        for i in range(PIECES):
            at = i * piece
            if r == 0:
                head = start_ref.at[0, :, at : at + piece]
                tail = start_ref.at[0, :, cells_here - halo + at : cells_here - halo + at + piece]
            else:
                head = wide.at[r, :, halo + at : halo + at + piece]
                tail = wide.at[r, :, cells_here + at : cells_here + at + piece]
            behind = halo + cells_here + at
            copies += [
                copy(head, r, slice(behind, behind + piece), season, left, 2 * i),
                copy(tail, r, slice(at, at + piece), season, right, 2 * i + 1),
            ]
        return copies

    def obs_copy(o):
        return pltpu.make_async_remote_copy(
            src_ref=obs.at[0],
            dst_ref=obs.at[o],
            send_sem=obs_send_sem.at[o],
            recv_sem=obs_recv_sem.at[o],
            device_id=(s, lax.rem(c + o, peers)),
            device_id_type=MESH,
        )

    sends = [halo_copies(r) for r in range(rounds)]
    body = copy(start_ref.at[0], 0, own, before, c, 2 * PIECES)

    pl.semaphore_wait(barrier, len(met))
    for one in sends[0]:
        one.start()
    body.start()

    @pl.loop(1, peers)
    def _(o):
        obs_copy(o).start()

    def pack(r, first, count):
        for t in range(first, first + count):
            v = wide[r, :, at_tile(t)]
            high = v.astype(BF16).astype(F32)
            packed[t] = jnp.concatenate([high, v - high], axis=0).astype(BF16)

    def gather_forcing():
        row_ids = lax.broadcasted_iota(jnp.int32, (force.shape[0], rows), 0).astype(F32)
        lane_ids = lax.broadcasted_iota(jnp.int32, (rows, rows), 0).astype(F32)
        here = c.astype(F32)
        force[...] = jnp.zeros_like(force)

        @pl.loop(0, peers)
        def _(o):
            @pl.when(o > 0)
            def _():
                obs_copy(o).wait_recv()

            block = obs[o]
            slots, values = [], []
            for i in range(lists):
                owner = block[i : i + 1]
                row = jnp.where(owner == here, block[lists + i : lists + i + 1], -1.0)
                lane = block[2 * lists + i : 2 * lists + i + 1]
                misfit = block[3 * lists + i : 3 * lists + i + 1]
                high = misfit.astype(BF16).astype(F32)
                hit = lane_ids == lane
                slots.append(jnp.where(row_ids == row, 1.0, 0.0).astype(BF16))
                values.append(
                    jnp.concatenate(
                        [jnp.where(hit, high, 0.0), jnp.where(hit, misfit - high, 0.0)], axis=0
                    ).astype(BF16)
                )
            force[...] += dot_nt(
                jnp.concatenate(slots, axis=1), jnp.concatenate(values, axis=1)
            )

    def at_tile(t):
        return slice(t * rows, (t + 1) * rows)

    def shifted(t):
        return slice(halo + t * rows, halo + (t + 1) * rows)

    def own_terms(r, day):
        matrix = r % 2
        pack(r, REACH, tiles_here)
        for t in range(tiles_here):
            v = wide[r, :, shifted(t)]
            both = dot_nt(packed[REACH + t], tiles_vm[matrix, t, 0])
            total = v + both[:tracers] + both[tracers:]
            if matrix == 1:
                at = (t * days + day) * tracers
                total += force[at : at + tracers, :rows] + force[at : at + tracers, rows:]
                for j in range(tracers):
                    total += jac_vm[day, j, :, at_tile(t)] * v[j : j + 1]
            base[:, at_tile(t)] = total

    def far_terms(r, chosen):
        matrix = r % 2
        for t in chosen:
            picks = []
            for k in range(1, near):
                ahead = cols_ref[0, k, matrix, t] + (total_tiles + REACH - c * tiles_here)
                if total_tiles & (total_tiles - 1) == 0:
                    ahead = ahead & (total_tiles - 1)
                else:
                    ahead = lax.rem(ahead, total_tiles)
                picks.append(packed[jnp.minimum(ahead, packed.shape[0] - 1)])
            stored = [tiles_vm[matrix, t, k] for k in range(1, near)]
            both = dot_nt(jnp.concatenate(picks, axis=1), jnp.concatenate(stored, axis=1))
            total = base[:, at_tile(t)] + both[:tracers] + both[tracers:]
            if r == rounds - 1:
                out_ref[:, at_tile(t)] = total
            else:
                wide[r + 1, :, shifted(t)] = total

    stores = [
        pltpu.make_async_copy(
            out_ref.at[:, i * halo : (i + 1) * halo],
            out_hbm.at[0, :, i * halo : (i + 1) * halo],
            store_sem.at[i],
        )
        for i in range(2)
    ]

    for r in range(rounds):
        day = days - 1 - r // 2
        if r == 0:
            body.wait_recv()
            loads[6].wait()
        if r == 1:
            loads[7].wait()
            loads[8].wait()
            gather_forcing()
        own_terms(r, day)
        if r == 0:
            loads[5].wait()
        for side in (0, 1):
            lands = REACH + tiles_here if side else 0
            from_tile = tiles_here - REACH if side else 0
            for i in range(PIECES):
                sends[r][2 * i + 1 - side].wait_recv()
                pack(r, lands + i * step, step)
            for i in range(PIECES):
                far_terms(r, range(from_tile + i * step, from_tile + (i + 1) * step))
                if r < rounds - 1:
                    sends[r + 1][2 * i + side].start()
            if r == rounds - 1:
                stores[side].start()

    for group in sends:
        for one in group:
            one.wait_send()
    for store in stores:
        store.wait()
    body.wait_send()

    @pl.loop(1, peers)
    def _(o):
        obs_copy(o).wait_send()


def on_device(
    seasons,
    peers,
    start_adjoint,
    adjoint_tiles,
    column_tiles,
    source_jacobian,
    obs_owner,
    obs_local,
    obs_day,
    obs_tracer,
    obs_misfit,
):
    days, tracers = source_jacobian.shape[1], source_jacobian.shape[2]
    tiles_here, near, rows = adjoint_tiles.shape[2], adjoint_tiles.shape[3], adjoint_tiles.shape[-1]
    cells_here = start_adjoint.shape[2]
    assert tiles_here == 2 * REACH
    wide_cells = cells_here + 2 * REACH * rows
    listed = obs_local.shape[1]
    rounds = 2 * days
    hbm = pl.BlockSpec(memory_space=pl.ANY)
    return pl.pallas_call(
        functools.partial(kernel, seasons, peers),
        out_shape=jax.ShapeDtypeStruct(start_adjoint.shape, F32),
        in_specs=[hbm] * 9,
        out_specs=hbm,
        scratch_shapes=[
            pltpu.SMEM((1, near, 2, tiles_here), jnp.int32),
        ]
        + [pltpu.VMEM((1, listed), jnp.int32)] * 4
        + [
            pltpu.VMEM((1, listed), F32),
            pltpu.VMEM((tracers, cells_here), F32),
            pltpu.VMEM((2, tiles_here, near, rows, rows), BF16),
            pltpu.VMEM((days, tracers, tracers, cells_here), F32),
            pltpu.VMEM((rounds, tracers, wide_cells), F32),
            pltpu.VMEM((tiles_here + 2 * REACH, 2 * tracers, rows), BF16),
            pltpu.VMEM((tracers, cells_here), F32),
            pltpu.VMEM((peers, 4 * listed // rows, rows), F32),
            pltpu.VMEM((tiles_here * days * tracers, 2 * rows), F32),
            pltpu.SemaphoreType.DMA((9,)),
            pltpu.SemaphoreType.DMA((2,)),
            pltpu.SemaphoreType.DMA((rounds, 2 * PIECES + 1)),
            pltpu.SemaphoreType.DMA((rounds, 2 * PIECES + 1)),
            pltpu.SemaphoreType.DMA((peers,)),
            pltpu.SemaphoreType.DMA((peers,)),
        ],
        compiler_params=pltpu.CompilerParams(collective_id=0, has_side_effects=True),
    )(
        column_tiles.transpose(0, 3, 1, 2),
        start_adjoint,
        adjoint_tiles,
        source_jacobian,
        obs_owner.reshape(1, listed),
        obs_local,
        obs_day,
        obs_tracer,
        obs_misfit,
    )


def solution(mesh):
    placed = (
        P("season", None, "cells"),
        P("season", None, "cells", None, None, None),
        P("season", None, "cells", None),
        P("season", None, None, None, "cells"),
        P("season", "cells", None),
        P("season", "cells"),
        P("season", "cells"),
        P("season", "cells"),
        P("season", "cells"),
    )
    return jax.shard_map(
        functools.partial(on_device, mesh.shape["season"], mesh.shape["cells"]),
        mesh=mesh,
        in_specs=placed,
        out_specs=P("season", None, "cells"),
        check_vma=False,
    )
```

```python
import functools

import jax
import jax.numpy as jnp
from jax import lax
from jax.experimental import pallas as pl
from jax.experimental.pallas import tpu as pltpu
from jax.sharding import PartitionSpec as P

REACH = 8
PIECES = 2
MESH = pl.DeviceIdType.MESH
F32 = jnp.float32
BF16 = jnp.bfloat16


def dot_nt(a, b):
    return lax.dot_general(a, b, (((1,), (1,)), ((), ())), preferred_element_type=F32)


def kernel(
    seasons,
    peers,
    cols_hbm,
    start_ref,
    tiles_hbm,
    jac_hbm,
    owner_hbm,
    local_hbm,
    day_hbm,
    tracer_hbm,
    misfit_hbm,
    out_hbm,
    cols_ref,
    owner_ref,
    local_ref,
    day_ref,
    tracer_ref,
    misfit_ref,
    out_ref,
    tiles_vm,
    jac_vm,
    wide,
    packed,
    base,
    obs,
    force,
    load_sem,
    store_sem,
    send_sem,
    recv_sem,
    obs_send_sem,
    obs_recv_sem,
):
    s = lax.axis_index("season")
    c = lax.axis_index("cells")
    days, tracers = jac_vm.shape[0], jac_vm.shape[1]
    tiles_here, near = tiles_vm.shape[1], tiles_vm.shape[2]
    rows = tiles_vm.shape[-1]
    cells_here = tiles_here * rows
    halo = REACH * rows
    total_tiles = tiles_here * peers
    piece = halo // PIECES
    step = REACH // PIECES
    rounds = 2 * days
    own = slice(halo, halo + cells_here)

    met = {(0, o) for o in range(1, peers)}
    met |= {(ds % seasons, dc % peers) for ds in (1, -1) for dc in (-1, 0, 1)}
    met = sorted(met - {(0, 0)})
    barrier = pltpu.get_barrier_semaphore()
    for ds, dc in met:
        pl.semaphore_signal(
            barrier,
            inc=1,
            device_id=(lax.rem(s + ds, seasons), lax.rem(c + dc, peers)),
            device_id_type=MESH,
        )

    pairs = (
        (owner_hbm, owner_ref),
        (local_hbm, local_ref),
        (day_hbm, day_ref),
        (tracer_hbm, tracer_ref),
        (misfit_hbm, misfit_ref),
        (cols_hbm, cols_ref),
        (tiles_hbm.at[0, 0], tiles_vm.at[0]),
        (tiles_hbm.at[0, 1], tiles_vm.at[1]),
        (jac_hbm.at[0], jac_vm),
    )
    loads = [pltpu.make_async_copy(a, b, load_sem.at[i]) for i, (a, b) in enumerate(pairs)]
    for load in loads:
        load.start()
    for load in loads[:5]:
        load.wait()

    shift = rows.bit_length() - 1
    local = local_ref[...]
    row_key = (local >> shift) * (days * tracers) + day_ref[...] * tracers + tracer_ref[...]
    fields = (
        owner_ref[...].astype(F32),
        row_key.astype(F32),
        (local & (rows - 1)).astype(F32),
        misfit_ref[...],
    )
    lists = local.shape[1] // rows
    pieces = [f[:, i * rows : (i + 1) * rows] for f in fields for i in range(lists)]
    obs[0] = jnp.concatenate(pieces, axis=0)

    left, right = lax.rem(c + peers - 1, peers), lax.rem(c + 1, peers)
    before = lax.rem(s + seasons - 1, seasons)

    def copy(src, r, lanes, season, cell, which):
        return pltpu.make_async_remote_copy(
            src_ref=src,
            dst_ref=wide.at[r, :, lanes],
            send_sem=send_sem.at[r, which],
            recv_sem=recv_sem.at[r, which],
            device_id=(season, cell),
            device_id_type=MESH,
        )

    def halo_copies(r):
        season = before if r == 0 else s
        copies = []
        for i in range(PIECES):
            at = i * piece
            if r == 0:
                head = start_ref.at[0, :, at : at + piece]
                tail = start_ref.at[0, :, cells_here - halo + at : cells_here - halo + at + piece]
            else:
                head = wide.at[r, :, halo + at : halo + at + piece]
                tail = wide.at[r, :, cells_here + at : cells_here + at + piece]
            behind = halo + cells_here + at
            copies += [
                copy(head, r, slice(behind, behind + piece), season, left, 2 * i),
                copy(tail, r, slice(at, at + piece), season, right, 2 * i + 1),
            ]
        return copies

    def obs_copy(o):
        return pltpu.make_async_remote_copy(
            src_ref=obs.at[0],
            dst_ref=obs.at[o],
            send_sem=obs_send_sem.at[o],
            recv_sem=obs_recv_sem.at[o],
            device_id=(s, lax.rem(c + o, peers)),
            device_id_type=MESH,
        )

    sends = [halo_copies(r) for r in range(rounds)]
    body = copy(start_ref.at[0], 0, own, before, c, 2 * PIECES)

    pl.semaphore_wait(barrier, len(met))
    for one in sends[0]:
        one.start()
    body.start()

    def pack(r, first, count):
        for t in range(first, first + count):
            v = wide[r, :, at_tile(t)]
            high = v.astype(BF16).astype(F32)
            packed[t] = jnp.concatenate([high, v - high], axis=0).astype(BF16)

    def gather_forcing():
        row_ids = lax.broadcasted_iota(jnp.int32, (force.shape[0], rows), 0).astype(F32)
        lane_ids = lax.broadcasted_iota(jnp.int32, (rows, rows), 0).astype(F32)
        here = c.astype(F32)
        force[...] = jnp.zeros_like(force)

        @pl.loop(0, peers)
        def _(o):
            @pl.when(o > 0)
            def _():
                obs_copy(o).wait_recv()

            block = obs[o]
            slots, values = [], []
            for i in range(lists):
                owner = block[i : i + 1]
                row = jnp.where(owner == here, block[lists + i : lists + i + 1], -1.0)
                lane = block[2 * lists + i : 2 * lists + i + 1]
                misfit = block[3 * lists + i : 3 * lists + i + 1]
                high = misfit.astype(BF16).astype(F32)
                hit = lane_ids == lane
                slots.append(jnp.where(row_ids == row, 1.0, 0.0).astype(BF16))
                values.append(
                    jnp.concatenate(
                        [jnp.where(hit, high, 0.0), jnp.where(hit, misfit - high, 0.0)], axis=0
                    ).astype(BF16)
                )
            force[...] += dot_nt(
                jnp.concatenate(slots, axis=1), jnp.concatenate(values, axis=1)
            )

    def at_tile(t):
        return slice(t * rows, (t + 1) * rows)

    def shifted(t):
        return slice(halo + t * rows, halo + (t + 1) * rows)

    def own_terms(r, day):
        matrix = r % 2
        pack(r, REACH, tiles_here)
        for t in range(tiles_here):
            v = wide[r, :, shifted(t)]
            both = dot_nt(packed[REACH + t], tiles_vm[matrix, t, 0])
            total = v + both[:tracers] + both[tracers:]
            if matrix == 1:
                at = (t * days + day) * tracers
                total += force[at : at + tracers, :rows] + force[at : at + tracers, rows:]
                for j in range(tracers):
                    total += jac_vm[day, j, :, at_tile(t)] * v[j : j + 1]
            base[:, at_tile(t)] = total

    def far_terms(r, chosen):
        matrix = r % 2
        for t in chosen:
            picks = []
            for k in range(1, near):
                ahead = cols_ref[0, k, matrix, t] + (total_tiles + REACH - c * tiles_here)
                if total_tiles & (total_tiles - 1) == 0:
                    ahead = ahead & (total_tiles - 1)
                else:
                    ahead = lax.rem(ahead, total_tiles)
                picks.append(packed[jnp.minimum(ahead, packed.shape[0] - 1)])
            stored = [tiles_vm[matrix, t, k] for k in range(1, near)]
            both = dot_nt(jnp.concatenate(picks, axis=1), jnp.concatenate(stored, axis=1))
            total = base[:, at_tile(t)] + both[:tracers] + both[tracers:]
            if r == rounds - 1:
                out_hbm[0, :, at_tile(t)] = total
            else:
                wide[r + 1, :, shifted(t)] = total

    for r in range(rounds):
        day = days - 1 - r // 2
        if r == 0:
            body.wait_recv()
            loads[6].wait()
        if r == 1:
            loads[7].wait()
            loads[8].wait()
            gather_forcing()
        own_terms(r, day)
        if r == 0:
            loads[5].wait()

            @pl.loop(1, peers)
            def _(o):
                obs_copy(o).start()

        for side in (0, 1):
            lands = REACH + tiles_here if side else 0
            from_tile = tiles_here - REACH if side else 0
            for i in range(PIECES):
                sends[r][2 * i + 1 - side].wait_recv()
                pack(r, lands + i * step, step)
            for i in range(PIECES):
                far_terms(r, range(from_tile + i * step, from_tile + (i + 1) * step))
                if r < rounds - 1:
                    sends[r + 1][2 * i + side].start()

    for group in sends:
        for one in group:
            one.wait_send()
    body.wait_send()

    @pl.loop(1, peers)
    def _(o):
        obs_copy(o).wait_send()


def on_device(
    seasons,
    peers,
    start_adjoint,
    adjoint_tiles,
    column_tiles,
    source_jacobian,
    obs_owner,
    obs_local,
    obs_day,
    obs_tracer,
    obs_misfit,
):
    days, tracers = source_jacobian.shape[1], source_jacobian.shape[2]
    tiles_here, near, rows = adjoint_tiles.shape[2], adjoint_tiles.shape[3], adjoint_tiles.shape[-1]
    cells_here = start_adjoint.shape[2]
    assert tiles_here == 2 * REACH
    wide_cells = cells_here + 2 * REACH * rows
    listed = obs_local.shape[1]
    rounds = 2 * days
    hbm = pl.BlockSpec(memory_space=pl.ANY)
    return pl.pallas_call(
        functools.partial(kernel, seasons, peers),
        out_shape=pltpu.VMEM(start_adjoint.shape, F32),
        in_specs=[hbm] * 9,
        out_specs=pl.BlockSpec(memory_space=pltpu.VMEM),
        scratch_shapes=[
            pltpu.SMEM((1, near, 2, tiles_here), jnp.int32),
        ]
        + [pltpu.VMEM((1, listed), jnp.int32)] * 4
        + [
            pltpu.VMEM((1, listed), F32),
            pltpu.VMEM((tracers, cells_here), F32),
            pltpu.VMEM((2, tiles_here, near, rows, rows), BF16),
            pltpu.VMEM((days, tracers, tracers, cells_here), F32),
            pltpu.VMEM((rounds, tracers, wide_cells), F32),
            pltpu.VMEM((tiles_here + 2 * REACH, 2 * tracers, rows), BF16),
            pltpu.VMEM((tracers, cells_here), F32),
            pltpu.VMEM((peers, 4 * listed // rows, rows), F32),
            pltpu.VMEM((tiles_here * days * tracers, 2 * rows), F32),
            pltpu.SemaphoreType.DMA((9,)),
            pltpu.SemaphoreType.DMA((2,)),
            pltpu.SemaphoreType.DMA((rounds, 2 * PIECES + 1)),
            pltpu.SemaphoreType.DMA((rounds, 2 * PIECES + 1)),
            pltpu.SemaphoreType.DMA((peers,)),
            pltpu.SemaphoreType.DMA((peers,)),
        ],
        compiler_params=pltpu.CompilerParams(collective_id=0, has_side_effects=True),
    )(
        column_tiles.transpose(0, 3, 1, 2),
        start_adjoint,
        adjoint_tiles,
        source_jacobian,
        obs_owner.reshape(1, listed),
        obs_local,
        obs_day,
        obs_tracer,
        obs_misfit,
    )


def solution(mesh):
    placed = (
        P("season", None, "cells"),
        P("season", None, "cells", None, None, None),
        P("season", None, "cells", None),
        P("season", None, None, None, "cells"),
        P("season", "cells", None),
        P("season", "cells"),
        P("season", "cells"),
        P("season", "cells"),
        P("season", "cells"),
    )
    return jax.shard_map(
        functools.partial(on_device, mesh.shape["season"], mesh.shape["cells"]),
        mesh=mesh,
        in_specs=placed,
        out_specs=P("season", None, "cells"),
        check_vma=False,
    )
```
